128 devices in a mesh: wide: 16 (over y_hi, z, core), narrow: 8 (over x, y_lo).
Axes of the slice: x: 4, y: 4 (y_hi: 2, y_lo: 2; y = y_hi * 2 + y_lo), z: 4, core: 2. Of those that a mesh axis runs over, the one named last changes fastest.
Arguments:
- density: float32 [128, 2, 512, 512], P(('wide', 'narrow')), may hold values from -6 to 6
- hamiltonian: bfloat16 [2, 512, 512], replicated, may hold values from -0.1875 to 0.1875
- left_operators: bfloat16 [7, 2, 512, 512], replicated, may hold values from -0.25 to 0.25
- right_operators: bfloat16 [7, 2, 512, 512], replicated, may hold values from -0.25 to 0.25
- block_mask: int32 [7, 2, 8, 8], replicated, may hold values 0 or 1
- operator_slot: int32 [7], replicated, may hold values from 0 to 6, each once
- flip_sign: int32 [7], replicated, may hold values from 0 to 1
- damping_rate: float32 [7], replicated, may hold values from 0.2 to 2
- lower_weight: float32 [7], replicated, may hold values from 0.5 to 2
Outputs:
- derivative: float32 [128, 2, 512, 512], P(('wide', 'narrow'))
The draws below stay inside these ranges and needn't reach their ends.
Inputs may be any that keep to these rules, and one draw needn't show every extreme that they name: `operator_slot`: each of the 7 slots is used by exactly one mode.
All inputs are finite; a program needn't handle non-finite values.
Results may differ from the reference program's by a relative error of at most 0.0023.
Values may be sent and summed in bfloat16 or wider, within the bound.
A program may use at most 128 MiB of HBM per device.

```python
import math
import jax
import jax.numpy as jnp
import numpy as np
from jax import lax

N = 512
BS = 64
MODES = 7
NB = 8
ADOS = 128


def with_ends(drawn, rng, smallest, largest):
    spot = [jax.random.randint(jax.random.fold_in(rng, axis), (), 0, length) for axis, length in enumerate(drawn.shape)]
    longest = drawn.shape.index(max(drawn.shape))
    next_to = spot[:longest] + [(spot[longest] + 1) % drawn.shape[longest]] + spot[longest + 1:]
    return drawn.at[tuple(spot)].set(smallest).at[tuple(next_to)].set(largest)


def shard_levels(own_key, shape, split, smallest, top_value):
    factor_of = 1.0
    for dim, shards_of in split:
        steps = jax.random.uniform(jax.random.fold_in(jax.random.fold_in(own_key, 6), dim), (shards_of,), jnp.float32, smallest / len(split), top_value / len(split))
        factor_of = factor_of * jnp.repeat(jnp.exp(steps), shape[dim] // shards_of).reshape((-1,) + (1,) * (len(shape) - 1 - dim))
    return factor_of


def noise(own_key, extent, width, most, shards=(), kind=jnp.bfloat16):
    values = width * jax.random.normal(own_key, extent, jnp.float32)
    if shards:
        values = values * shard_levels(own_key, extent, shards, -0.22, 0.18)
    return jnp.clip(values, -most, most).astype(kind)


def setup_inputs(seed: int = 0) -> dict:
    splits = jax.random.split(jax.random.key(seed), 10)
    return {
        "density": noise(splits[0], (ADOS, 2, N, N), 1.0, 6.0, ((0, 128),), jnp.float32),
        "hamiltonian": noise(splits[1], (2, N, N), (2 * N) ** -0.5, 0.1875),
        "left_operators": noise(splits[2], (MODES, 2, N, N), N ** -0.5, 0.25),
        "right_operators": noise(splits[3], (MODES, 2, N, N), N ** -0.5, 0.25),
        "block_mask": with_ends((jax.random.randint(splits[4], (MODES, 2, NB, NB), 0, 8) < 3).astype(jnp.int32), jax.random.fold_in(splits[4], 1), 0, 1),
        "operator_slot": jax.random.permutation(splits[5], MODES).astype(jnp.int32),
        "flip_sign": with_ends(jax.random.randint(splits[6], (MODES,), 0, 2), jax.random.fold_in(splits[6], 1), 0, 1).astype(jnp.int32),
        "damping_rate": jnp.clip(jnp.exp(jax.random.uniform(splits[7], (MODES,), jnp.float32, math.log(0.2), math.log(2.0))), 0.2, 2.0),
        "lower_weight": jnp.clip(jnp.exp(jax.random.uniform(splits[8], (MODES,), jnp.float32, math.log(0.5), math.log(2.0))), 0.5, 2.0),
    }


def left_product(operator, batch):
    first = operator.astype(jnp.float32)
    second = batch.astype(jnp.float32)
    high = lax.Precision.HIGHEST
    real = jnp.einsum("ij,ljk->lik", first[0], second[:, 0], precision=high) - jnp.einsum("ij,ljk->lik", first[1], second[:, 1], precision=high)
    imag = jnp.einsum("ij,ljk->lik", first[0], second[:, 1], precision=high) + jnp.einsum("ij,ljk->lik", first[1], second[:, 0], precision=high)
    return jnp.stack([real, imag], axis=1)


def right_product(batch, operator):
    first = batch.astype(jnp.float32)
    second = operator.astype(jnp.float32)
    high = lax.Precision.HIGHEST
    real = jnp.einsum("lij,jk->lik", first[:, 0], second[0], precision=high) - jnp.einsum("lij,jk->lik", first[:, 1], second[1], precision=high)
    imag = jnp.einsum("lij,jk->lik", first[:, 0], second[1], precision=high) + jnp.einsum("lij,jk->lik", first[:, 1], second[0], precision=high)
    return jnp.stack([real, imag], axis=1)


def reference(density, hamiltonian, left_operators, right_operators, block_mask, operator_slot, flip_sign, damping_rate, lower_weight):
    indices = np.arange(ADOS)
    bit_table = (indices[:, None] >> np.arange(MODES)[None, :]) & 1
    expanded = jnp.repeat(jnp.repeat(block_mask, BS, axis=2), BS, axis=3).astype(jnp.bfloat16)
    left_masked = left_operators * expanded[:, 0][:, None]
    right_masked = right_operators * expanded[:, 1][:, None]
    rounded = density.astype(jnp.bfloat16)
    commutator = left_product(hamiltonian, rounded) - right_product(rounded, hamiltonian)
    result = jnp.stack([commutator[:, 1], -commutator[:, 0]], axis=1)
    occupied = jnp.asarray(bit_table, dtype=jnp.float32)
    rates = jnp.sum(occupied * damping_rate[None, :], axis=1)
    result = result - rates[:, None, None, None] * density
    for flip_mode in range(MODES):
        partner = rounded[indices ^ (1 << flip_mode)]
        slot = operator_slot[flip_mode]
        term = left_product(left_masked[slot], partner) + right_product(partner, right_masked[slot])
        below = bit_table[:, :flip_mode].sum(axis=1) % 2
        parity = jnp.asarray(1 - 2 * below, dtype=jnp.float32)
        sign_value = (1 - 2 * flip_sign[flip_mode]).astype(jnp.float32)
        weight = jnp.where(occupied[:, flip_mode] > 0.5, lower_weight[flip_mode], jnp.float32(1.0))
        coef = parity * sign_value * weight
        result = result + coef[:, None, None, None] * term
    return result
```

```python
import functools

import jax
import jax.numpy as jnp
from jax import lax
from jax.experimental import pallas as pl
from jax.experimental.pallas import tpu as pltpu
from jax.sharding import PartitionSpec as P

MESH = pl.DeviceIdType.MESH
F32, BF16 = jnp.float32, jnp.bfloat16
N, BS, MODES, NB = 512, 64, 7, 8
CH = 128
NC = N // CH
SUB = 32
NS = N // SUB
PER = CH // SUB
OWN = MODES
RINGS = (
    (0, 6, (0, 1), (8, 1)),
    (1, 2, (0, 2), (0, 6)),
    (4, 5, (2, 0), (6, 0)),
)
CORE = 3


def kernel(
    slot_ref, flip_ref, rate_ref, lower_ref, mask_ref, dens_hbm, ham_hbm, left_hbm, right_hbm, out_hbm,
    rho, left, right, ham, acc, rows_ref, coef, out_sem, dens_sem, ham_sem, left_sem, right_sem, send_sem, recv_sem,
):
    wide, narrow = lax.axis_index("wide"), lax.axis_index("narrow")
    index = wide * 8 + narrow

    def peer(masks):
        return (wide ^ masks[0], narrow ^ masks[1])

    dens = [
        pltpu.make_async_copy(
            dens_hbm.at[0, :, pl.ds(c * CH, CH), :], acc.at[:, pl.ds(c * CH, CH), :], dens_sem.at[c])
        for c in range(NC)
    ]
    for copy in dens:
        copy.start()
    ham_copy = pltpu.make_async_copy(ham_hbm, ham, ham_sem)
    ham_copy.start()
    loads = []
    for s in range(MODES):
        loads.append((
            pltpu.make_async_copy(left_hbm.at[s], left.at[s], left_sem.at[s]),
            pltpu.make_async_copy(right_hbm.at[s], right.at[s], right_sem.at[s]),
        ))
    for pair in loads:
        for copy in pair:
            copy.start()

    barrier = pltpu.get_barrier_semaphore()
    peers = [(1, 0)] + [m for r in RINGS for m in r[2:]]
    for masks in peers:
        pl.semaphore_signal(barrier, inc=1, device_id=peer(masks), device_id_type=MESH)

    rate = jnp.float32(0.0)
    below = jnp.int32(0)
    for k in range(MODES):
        bit = (index // 2**k) % 2
        parity = (1 - 2 * (below % 2)).astype(F32)
        sign = (1 - 2 * flip_ref[k]).astype(F32)
        on = bit.astype(F32)
        coef[k] = parity * sign * (on * lower_ref[k] + (1.0 - on))
        rate = rate + on * rate_ref[k]
        below = below + bit
    coef[OWN] = jnp.float32(1.0)

    spread = (
        lax.broadcasted_iota(jnp.int32, (NB, N), 1) // BS == lax.broadcasted_iota(jnp.int32, (NB, N), 0)
    ).astype(F32)
    for s in range(MODES):
        for side in range(2):
            rows_ref[s, side] = jnp.dot(mask_ref[s, side].astype(F32), spread, preferred_element_type=F32)

    def send(k, s, masks, src):
        at = (s // PER, slice(None), pl.ds(pl.multiple_of((s % PER) * SUB, SUB), SUB), slice(None))
        return pltpu.make_async_remote_copy(
            src_ref=rho.at[(src,) + at], dst_ref=rho.at[(k,) + at],
            send_sem=send_sem.at[k, s], recv_sem=recv_sem.at[k, s],
            device_id=peer(masks), device_id_type=MESH)

    def send_own(s):
        for low, _, near, _ in RINGS:
            send(low, s, near, OWN).start()
        send(CORE, s, (1, 0), OWN).start()

    def forward(s):
        for low, high, near, far in RINGS:
            send(low, s, near, OWN).wait_recv()
            send(high, s, far, low).start()

    for c in range(NC):
        dens[c].wait()
        rows = pl.ds(c * CH, CH)
        value = acc[:, rows, :]
        rho[OWN, c] = value.astype(BF16)
        acc[:, rows, :] = (-rate) * value
        if c == 0:
            pl.semaphore_wait(barrier, len(peers))
        else:
            for s in range((c - 1) * PER, c * PER):
                send_own(s)
    ham_copy.wait()
    left[OWN, 0] = ham[1]
    left[OWN, 1] = -ham[0]
    right[OWN, 0] = -ham[1]
    right[OWN, 1] = ham[0]
    for s in range((NC - 1) * PER, NS):
        send_own(s)

    def step(k, slot, c):
        rows = pl.ds(pl.multiple_of(c * CH, CH), CH)
        weight = coef[k]
        real, imag = rho[k, c, 0], rho[k, c, 1]
        both = jnp.concatenate([real, imag], axis=0)
        lr, li = left[slot, 0, :, rows], left[slot, 1, :, rows]
        acc[0] += weight * jnp.dot(jnp.concatenate([lr, -li], axis=1), both, preferred_element_type=F32)
        acc[1] += weight * jnp.dot(jnp.concatenate([li, lr], axis=1), both, preferred_element_type=F32)
        wide_rows = jnp.concatenate([
            jnp.concatenate([real, -imag], axis=1), jnp.concatenate([imag, real], axis=1)], axis=0)
        ops = jnp.concatenate([right[slot, 0], right[slot, 1]], axis=0)
        value = jnp.dot(wide_rows, ops, preferred_element_type=F32)
        acc[0, rows, :] += weight * value[:CH]
        acc[1, rows, :] += weight * value[CH:]

    @pl.loop(0, NC)
    def _(c):
        step(OWN, OWN, c)

    forward(0)
    for s in range(MODES):
        for copy in loads[s]:
            copy.wait()

        @pl.loop(0, NB)
        def _(i):
            rows = pl.ds(pl.multiple_of(i * BS, BS), BS)
            for side, ops in ((0, left), (1, right)):
                keep = rows_ref[s, side, pl.ds(i, 1), :].astype(BF16)
                ops[s, 0, rows, :] = ops[s, 0, rows, :] * keep
                ops[s, 1, rows, :] = ops[s, 1, rows, :] * keep

        if s % 3 == 2:
            forward(1 + s // 3)

    @pl.loop(0, NC)
    def _(c):
        for s in range(PER):
            send(CORE, c * PER + s, (1, 0), OWN).wait_recv()
        step(CORE, slot_ref[CORE], c)

        @pl.when(c % 2 == 1)
        def _():
            forward(3 + c // 2)

    done = 5
    for c in range(NC):
        for r, (low, high, near, far) in enumerate(RINGS):
            while done < (c + 1) * PER or done < min(NS, (c + 1) * PER + r):
                forward(done)
                done += 1
            step(low, slot_ref[low], c)
        for low, high, near, far in RINGS:
            if done < min(NS, (c + 2) * PER) :
                forward(done)
                done += 1
            for s in range(c * PER, (c + 1) * PER):
                send(high, s, far, low).wait_recv()
            step(high, slot_ref[high], c)

    out = pltpu.make_async_copy(acc, out_hbm.at[0], out_sem)
    out.start()
    for s in range(NS):
        for low, high, near, far in RINGS:
            send(low, s, near, OWN).wait_send()
            send(high, s, far, low).wait_send()
        send(CORE, s, (1, 0), OWN).wait_send()
    out.wait()


def body(density, hamiltonian, left_operators, right_operators, block_mask, operator_slot, flip_sign, damping_rate, lower_weight):
    smem, vmem, anywhere = (pl.BlockSpec(memory_space=m) for m in (pltpu.SMEM, pltpu.VMEM, pl.ANY))
    return pl.pallas_call(
        kernel,
        out_shape=jax.ShapeDtypeStruct((1, 2, N, N), F32),
        in_specs=[smem] * 4 + [vmem] + [anywhere] * 4,
        out_specs=anywhere,
        scratch_shapes=[
            pltpu.VMEM((MODES + 1, NC, 2, CH, N), BF16),
            pltpu.VMEM((MODES + 1, 2, N, N), BF16),
            pltpu.VMEM((MODES + 1, 2, N, N), BF16),
            pltpu.VMEM((2, N, N), BF16),
            pltpu.VMEM((2, N, N), F32),
            pltpu.VMEM((MODES, 2, NB, N), F32),
            pltpu.SMEM((MODES + 1,), F32),
            pltpu.SemaphoreType.DMA,
            pltpu.SemaphoreType.DMA((NC,)),
            pltpu.SemaphoreType.DMA,
            pltpu.SemaphoreType.DMA((MODES,)),
            pltpu.SemaphoreType.DMA((MODES,)),
            pltpu.SemaphoreType.DMA((MODES, NS)),
            pltpu.SemaphoreType.DMA((MODES, NS)),
        ],
        compiler_params=pltpu.CompilerParams(
            collective_id=0, has_side_effects=True, vmem_limit_bytes=60 * 1024 * 1024),
        name="heom",
    )(operator_slot, flip_sign, damping_rate, lower_weight, block_mask, density, hamiltonian, left_operators, right_operators)


def solution(mesh):
    placed = (P(("wide", "narrow"), None, None, None), P(), P(), P(), P(), P(), P(), P(), P())
    return jax.shard_map(
        body, mesh=mesh, in_specs=placed, out_specs=P(("wide", "narrow"), None, None, None), check_vma=False)
```

```python
import jax
import jax.numpy as jnp
from jax import lax
from jax.experimental import pallas as pl
from jax.experimental.pallas import tpu as pltpu
from jax.sharding import PartitionSpec as P

MESH = pl.DeviceIdType.MESH
F32, BF16 = jnp.float32, jnp.bfloat16
N, BS, MODES, NB = 512, 64, 7, 8
CH = 128
NC = N // CH
SUB = 64
NS = N // SUB
PER = CH // SUB
MODE_AT = (0, 1, 4, 6, 2, 5, 3)
CORE, OWN = 6, 7
NEAR = ((0, 1), (0, 2), (2, 0))
FAR = ((8, 1), (0, 6), (6, 0))
OTHER = (1, 0)
RINGS = range(3)


def plan():
    def forward(s):
        return [("forward", None, s)]

    def steps(places, c):
        return [("step", p, c) for p in places]

    near, far = (0, 1, 2), (3, 4, 5)
    out = [("step", OWN, c) for c in range(NC)] + forward(0)
    out += [("mask", None, s) for s in range(MODES)]
    out += steps([CORE], 0) + forward(1) + steps([CORE], 1) + steps([CORE], 2) + steps([CORE], 3) + forward(2)
    out += steps(near, 0) + forward(3)
    out += steps(near, 1) + steps(far[:1], 0) + forward(4)
    out += steps(far[1:], 0) + forward(5)
    out += steps(near, 2) + forward(6)
    out += steps(far, 1) + forward(7)
    out += steps(near, 3) + steps(far, 2) + steps(far, 3)
    return out


PLAN = plan()


def kernel(
    slot_hbm, flip_hbm, rate_hbm, lower_hbm, mask_hbm, dens_hbm, ham_hbm, left_hbm, right_hbm, out_ref,
    rho, left, right, ham, rows_ref, coef, slot_at, slot_ref, flip_ref, rate_ref, lower_ref, mask_ref,
    small_sem, dens_sem, ham_sem, left_sem, right_sem, send_sem, recv_sem,
):
    wide, narrow = lax.axis_index("wide"), lax.axis_index("narrow")
    index = wide * 8 + narrow
    acc = out_ref.at[0]

    def peer(masks):
        return (wide ^ masks[0], narrow ^ masks[1])

    barrier = pltpu.get_barrier_semaphore()
    peers = (OTHER,) + NEAR + FAR
    for masks in peers:
        pl.semaphore_signal(barrier, inc=1, device_id=peer(masks), device_id_type=MESH)

    dens = [
        pltpu.make_async_copy(
            dens_hbm.at[0, :, pl.ds(s * SUB, SUB), :], acc.at[:, pl.ds(s * SUB, SUB), :], dens_sem.at[s])
        for s in range(NS)
    ]
    for copy in dens:
        copy.start()
    small = [
        pltpu.make_async_copy(src, dst, small_sem.at[i])
        for i, (src, dst) in enumerate((
            (rate_hbm, rate_ref), (flip_hbm, flip_ref), (lower_hbm, lower_ref), (slot_hbm, slot_ref), (mask_hbm, mask_ref)))
    ]
    for copy in small:
        copy.start()
    ham_copy = pltpu.make_async_copy(ham_hbm, ham, ham_sem)
    ham_copy.start()

    def load(s):
        return (
            pltpu.make_async_copy(left_hbm.at[s], left.at[s], left_sem.at[s]),
            pltpu.make_async_copy(right_hbm.at[s], right.at[s], right_sem.at[s]),
        )

    for copy in small[:4]:
        copy.wait()
    rate = jnp.float32(0.0)
    below = jnp.int32(0)
    for k in range(MODES):
        place = MODE_AT.index(k)
        bit = (index // 2**k) % 2
        parity = (1 - 2 * (below % 2)).astype(F32)
        sign = (1 - 2 * flip_ref[k]).astype(F32)
        on = bit.astype(F32)
        coef[place] = parity * sign * (on * lower_ref[k] + (1.0 - on))
        slot_at[place] = slot_ref[k]
        rate = rate + on * rate_ref[k]
        below = below + bit
    coef[OWN] = jnp.float32(1.0)

    def send(place, s, masks, src):
        return pltpu.make_async_remote_copy(
            src_ref=rho.at[src, s], dst_ref=rho.at[place, s],
            send_sem=send_sem.at[place, s], recv_sem=recv_sem.at[place, s],
            device_id=peer(masks), device_id_type=MESH)

    def send_own(s):
        for r in RINGS:
            send(r, s, NEAR[r], OWN).start()
        send(CORE, s, OTHER, OWN).start()

    def forward(s):
        for r in RINGS:
            send(r, s, NEAR[r], OWN).wait_recv()
            send(3 + r, s, FAR[r], r).start()

    for s in range(NS):
        dens[s].wait()
        rows = pl.ds(s * SUB, SUB)
        value = acc[:, rows, :]
        rho[OWN, s] = value.astype(BF16)
        acc[:, rows, :] = (-rate) * value
        if s == 0:
            pl.semaphore_wait(barrier, len(peers))
        else:
            send_own(s - 1)
        if s == NS // 2:
            for i in range(MODES):
                for copy in load(i):
                    copy.start()
    ham_copy.wait()
    left[OWN, 0] = ham[1]
    left[OWN, 1] = -ham[0]
    right[OWN, 0] = -ham[1]
    right[OWN, 1] = ham[0]
    send_own(NS - 1)

    small[4].wait()
    spread = (
        lax.broadcasted_iota(jnp.int32, (NB, N), 1) // BS == lax.broadcasted_iota(jnp.int32, (NB, N), 0)
    ).astype(F32)

    rows_ref[...] = jnp.dot(
        mask_ref[...].reshape(MODES * 2 * NB, NB).astype(F32), spread, preferred_element_type=F32
    ).reshape(MODES, 2, NB, N)

    def left_part(place, c):
        slot, weight = OWN if place == OWN else slot_at[place], coef[place]
        rows = pl.ds(c * CH, CH)
        both = jnp.concatenate([rho[place, c * PER + s, i] for i in range(2) for s in range(PER)], axis=0)
        lr, li = left[slot, 0, :, rows], left[slot, 1, :, rows]
        acc[0] += weight * jnp.dot(jnp.concatenate([lr, -li], axis=1), both, preferred_element_type=F32)
        acc[1] += weight * jnp.dot(jnp.concatenate([li, lr], axis=1), both, preferred_element_type=F32)

    def right_part(place, first, count):
        slot, weight = OWN if place == OWN else slot_at[place], coef[place]
        rows = pl.ds(first * SUB, count * SUB)
        real, imag = (jnp.concatenate([rho[place, first + s, i] for s in range(count)], axis=0) for i in range(2))
        wide_rows = jnp.concatenate([
            jnp.concatenate([real, -imag], axis=1), jnp.concatenate([imag, real], axis=1)], axis=0)
        ops = jnp.concatenate([right[slot, 0], right[slot, 1]], axis=0)
        value = jnp.dot(wide_rows, ops, preferred_element_type=F32)
        acc[0, rows, :] += weight * value[: count * SUB]
        acc[1, rows, :] += weight * value[count * SUB :]

    def step(place, c):
        left_part(place, c)
        right_part(place, c * PER, PER)

    def mask(s):
        for copy in load(s):
            copy.wait()
        for i in range(NB):
            rows = pl.ds(i * BS, BS)
            for side, ops in ((0, left), (1, right)):
                keep = rows_ref[s, side, i : i + 1, :].astype(BF16)
                ops[s, 0, rows, :] = ops[s, 0, rows, :] * keep
                ops[s, 1, rows, :] = ops[s, 1, rows, :] * keep

    def arrived(place, s):
        if place == CORE:
            send(CORE, s, OTHER, OWN).wait_recv()
        elif place >= 3 and place != OWN:
            send(place, s, FAR[place - 3], place - 3).wait_recv()

    for what, place, c in PLAN:
        if what == "forward":
            forward(c)
        elif what == "mask":
            mask(c)
        elif what == "step":
            for s in range(c * PER, (c + 1) * PER):
                arrived(place, s)
            step(place, c)
        elif what == "right":
            arrived(place, c)
            right_part(place, c, 1)
        else:
            left_part(place, c)

    @pl.loop(0, NS)
    def _(s):
        for r in RINGS:
            send(r, s, NEAR[r], OWN).wait_send()
            send(3 + r, s, FAR[r], r).wait_send()
        send(CORE, s, OTHER, OWN).wait_send()


def body(density, hamiltonian, left_operators, right_operators, block_mask, operator_slot, flip_sign, damping_rate, lower_weight):
    vmem, anywhere = (pl.BlockSpec(memory_space=m) for m in (pltpu.VMEM, pl.ANY))
    return pl.pallas_call(
        kernel,
        out_shape=pltpu.VMEM((1, 2, N, N), F32),
        in_specs=[anywhere] * 9,
        out_specs=vmem,
        scratch_shapes=[
            pltpu.VMEM((MODES + 1, NS, 2, SUB, N), BF16),
            pltpu.VMEM((MODES + 1, 2, N, N), BF16),
            pltpu.VMEM((MODES + 1, 2, N, N), BF16),
            pltpu.VMEM((2, N, N), BF16),
            pltpu.VMEM((MODES, 2, NB, N), F32),
            pltpu.SMEM((MODES + 1,), F32),
            pltpu.SMEM((MODES + 1,), jnp.int32),
            pltpu.SMEM((MODES,), jnp.int32),
            pltpu.SMEM((MODES,), jnp.int32),
            pltpu.SMEM((MODES,), F32),
            pltpu.SMEM((MODES,), F32),
            pltpu.VMEM((MODES, 2, NB, NB), jnp.int32),
            pltpu.SemaphoreType.DMA((5,)),
            pltpu.SemaphoreType.DMA((NS,)),
            pltpu.SemaphoreType.DMA,
            pltpu.SemaphoreType.DMA((MODES,)),
            pltpu.SemaphoreType.DMA((MODES,)),
            pltpu.SemaphoreType.DMA((MODES, NS)),
            pltpu.SemaphoreType.DMA((MODES, NS)),
        ],
        compiler_params=pltpu.CompilerParams(
            collective_id=0, has_side_effects=True, vmem_limit_bytes=58 * 1024 * 1024),
        name="heom",
    )(operator_slot, flip_sign, damping_rate, lower_weight, block_mask, density, hamiltonian, left_operators, right_operators)


def solution(mesh):
    placed = (P(("wide", "narrow"), None, None, None), P(), P(), P(), P(), P(), P(), P(), P())
    return jax.shard_map(
        body, mesh=mesh, in_specs=placed, out_specs=P(("wide", "narrow"), None, None, None), check_vma=False)
```

```python
import jax
import jax.numpy as jnp
from jax import lax
from jax.experimental import pallas as pl
from jax.experimental.pallas import tpu as pltpu
from jax.sharding import PartitionSpec as P

MESH = pl.DeviceIdType.MESH
F32, BF16 = jnp.float32, jnp.bfloat16
N, BS, MODES, NB = 512, 64, 7, 8
CH = 128
NC = N // CH
SUB = 64
NS = N // SUB
PER = CH // SUB
MODE_AT = (0, 1, 4, 6, 2, 5, 3)
CORE, OWN = 6, 7
NEAR = ((0, 1), (0, 2), (2, 0))
FAR = ((8, 1), (0, 6), (6, 0))
OTHER = (1, 0)
LAST = NS - 1
ORDER = (0, LAST) + tuple(range(1, LAST))
RINGS = range(3)


def plan():
    def forward(s):
        return [("forward", None, s)]

    def steps(places, c):
        return [("step", p, c) for p in places]

    def group(places, c):
        return [("group", places, c)]

    near, far = (0, 1, 2), (3, 4, 5)
    out = [("step", OWN, c) for c in range(NC)] + forward(0)
    out += [("mask", None, s) for s in range(MODES)]
    out += steps([CORE], 0) + forward(1) + [("relay", None, LAST)]
    out += steps([CORE], 1) + steps([CORE], 2) + steps([CORE], 3) + forward(2)
    out += group(near, 0) + forward(3)
    out += group(near, 1) + steps(far[:1], 0) + forward(4)
    out += group(far[1:], 0) + forward(5)
    out += group(near, 2) + steps(far[:1], 1) + forward(6)
    out += group(far[1:], 1) + forward(7)
    out += group(near, 3) + group(far, 2) + group(far, 3)
    return out


PLAN = plan()


def kernel(
    slot_hbm, flip_hbm, rate_hbm, lower_hbm, mask_hbm, dens_hbm, ham_hbm, left_hbm, right_hbm, out_ref,
    rho, relay, left, right, ham, rows_ref, coef, slot_at, slot_ref, flip_ref, rate_ref, lower_ref, mask_ref,
    small_sem, dens_sem, ham_sem, left_sem, right_sem, send_sem, recv_sem, relay_send, relay_recv,
):
    wide, narrow = lax.axis_index("wide"), lax.axis_index("narrow")
    index = wide * 8 + narrow
    acc = out_ref.at[0]

    def peer(masks):
        return (wide ^ masks[0], narrow ^ masks[1])

    barrier = pltpu.get_barrier_semaphore()
    peers = (OTHER,) + NEAR + FAR
    for masks in peers:
        pl.semaphore_signal(barrier, inc=1, device_id=peer(masks), device_id_type=MESH)

    dens = [
        pltpu.make_async_copy(
            dens_hbm.at[0, :, pl.ds(s * SUB, SUB), :], acc.at[:, pl.ds(s * SUB, SUB), :], dens_sem.at[s])
        for s in range(NS)
    ]
    for s in ORDER:
        dens[s].start()
    small = [
        pltpu.make_async_copy(src, dst, small_sem.at[i])
        for i, (src, dst) in enumerate((
            (rate_hbm, rate_ref), (flip_hbm, flip_ref), (lower_hbm, lower_ref), (slot_hbm, slot_ref), (mask_hbm, mask_ref)))
    ]
    for copy in small:
        copy.start()
    ham_copy = pltpu.make_async_copy(ham_hbm, ham, ham_sem)
    ham_copy.start()

    def load(s):
        return (
            pltpu.make_async_copy(left_hbm.at[s], left.at[s], left_sem.at[s]),
            pltpu.make_async_copy(right_hbm.at[s], right.at[s], right_sem.at[s]),
        )

    for copy in small[:4]:
        copy.wait()
    rate = jnp.float32(0.0)
    below = jnp.int32(0)
    for k in range(MODES):
        place = MODE_AT.index(k)
        bit = (index // 2**k) % 2
        parity = (1 - 2 * (below % 2)).astype(F32)
        sign = (1 - 2 * flip_ref[k]).astype(F32)
        on = bit.astype(F32)
        coef[place] = parity * sign * (on * lower_ref[k] + (1.0 - on))
        slot_at[place] = slot_ref[k]
        rate = rate + on * rate_ref[k]
        below = below + bit
    coef[OWN] = jnp.float32(1.0)

    def send(place, s, masks, src):
        return pltpu.make_async_remote_copy(
            src_ref=rho.at[src, s], dst_ref=rho.at[place, s],
            send_sem=send_sem.at[place, s], recv_sem=recv_sem.at[place, s],
            device_id=peer(masks), device_id_type=MESH)

    def pass_by(r):
        return pltpu.make_async_remote_copy(
            src_ref=rho.at[OWN, LAST], dst_ref=relay.at[r], send_sem=relay_send.at[r], recv_sem=relay_recv.at[r],
            device_id=peer(FAR[r]), device_id_type=MESH)

    def pass_on(r):
        return pltpu.make_async_remote_copy(
            src_ref=relay.at[r], dst_ref=rho.at[3 + r, LAST],
            send_sem=send_sem.at[3 + r, LAST], recv_sem=recv_sem.at[3 + r, LAST],
            device_id=peer(NEAR[r]), device_id_type=MESH)

    def send_near(s):
        for r in RINGS:
            send(r, s, NEAR[r], OWN).start()
        send(CORE, s, OTHER, OWN).start()

    def send_own(s):
        if s == LAST:
            for r in RINGS:
                pass_by(r).start()
        else:
            send_near(s)

    def forward(s):
        for r in RINGS:
            send(r, s, NEAR[r], OWN).wait_recv()
            if s != LAST:
                send(3 + r, s, FAR[r], r).start()

    for i, s in enumerate(ORDER):
        dens[s].wait()
        rows = pl.ds(s * SUB, SUB)
        value = acc[:, rows, :]
        rho[OWN, s] = value.astype(BF16)
        acc[:, rows, :] = (-rate) * value
        if i == 0:
            pl.semaphore_wait(barrier, len(peers))
        else:
            send_own(ORDER[i - 1])
        if i == NS // 2:
            for j in range(MODES):
                for copy in load(j):
                    copy.start()
    ham_copy.wait()
    left[OWN, 0] = ham[1]
    left[OWN, 1] = -ham[0]
    right[OWN, 0] = -ham[1]
    right[OWN, 1] = ham[0]
    send_own(ORDER[-1])
    send_near(LAST)

    small[4].wait()
    spread = (
        lax.broadcasted_iota(jnp.int32, (NB, N), 1) // BS == lax.broadcasted_iota(jnp.int32, (NB, N), 0)
    ).astype(F32)

    rows_ref[...] = jnp.dot(
        mask_ref[...].reshape(MODES * 2 * NB, NB).astype(F32), spread, preferred_element_type=F32
    ).reshape(MODES, 2, NB, N)

    def left_part(place, c):
        slot, weight = OWN if place == OWN else slot_at[place], coef[place]
        rows = pl.ds(c * CH, CH)
        both = jnp.concatenate([rho[place, c * PER + s, i] for i in range(2) for s in range(PER)], axis=0)
        lr, li = left[slot, 0, :, rows], left[slot, 1, :, rows]
        acc[0] += weight * jnp.dot(jnp.concatenate([lr, -li], axis=1), both, preferred_element_type=F32)
        acc[1] += weight * jnp.dot(jnp.concatenate([li, lr], axis=1), both, preferred_element_type=F32)

    def left_group(places, c):
        rows = pl.ds(c * CH, CH)
        real, imag = 0.0, 0.0
        for place in places:
            slot, weight = slot_at[place], coef[place]
            both = jnp.concatenate([rho[place, c * PER + s, i] for i in range(2) for s in range(PER)], axis=0)
            lr, li = left[slot, 0, :, rows], left[slot, 1, :, rows]
            real += weight * jnp.dot(jnp.concatenate([lr, -li], axis=1), both, preferred_element_type=F32)
            imag += weight * jnp.dot(jnp.concatenate([li, lr], axis=1), both, preferred_element_type=F32)
        acc[0] += real
        acc[1] += imag

    def right_part(place, first, count):
        slot, weight = OWN if place == OWN else slot_at[place], coef[place]
        rows = pl.ds(first * SUB, count * SUB)
        real, imag = (jnp.concatenate([rho[place, first + s, i] for s in range(count)], axis=0) for i in range(2))
        wide_rows = jnp.concatenate([
            jnp.concatenate([real, -imag], axis=1), jnp.concatenate([imag, real], axis=1)], axis=0)
        ops = jnp.concatenate([right[slot, 0], right[slot, 1]], axis=0)
        value = jnp.dot(wide_rows, ops, preferred_element_type=F32)
        acc[0, rows, :] += weight * value[: count * SUB]
        acc[1, rows, :] += weight * value[count * SUB :]

    def step(place, c):
        left_part(place, c)
        right_part(place, c * PER, PER)

    def mask(s):
        for copy in load(s):
            copy.wait()
        for i in range(NB):
            rows = pl.ds(i * BS, BS)
            for side, ops in ((0, left), (1, right)):
                keep = rows_ref[s, side, i : i + 1, :].astype(BF16)
                ops[s, 0, rows, :] = ops[s, 0, rows, :] * keep
                ops[s, 1, rows, :] = ops[s, 1, rows, :] * keep

    def arrived(place, s):
        if place == CORE:
            send(CORE, s, OTHER, OWN).wait_recv()
        elif place >= 3 and place != OWN:
            send(place, s, FAR[place - 3], place - 3).wait_recv()

    for what, place, c in PLAN:
        if what == "forward":
            forward(c)
        elif what == "relay":
            for r in RINGS:
                pass_by(r).wait_recv()
                pass_on(r).start()
        elif what == "mask":
            mask(c)
        elif what == "step":
            for s in range(c * PER, (c + 1) * PER):
                arrived(place, s)
            step(place, c)
        else:
            for p in place:
                for s in range(c * PER, (c + 1) * PER):
                    arrived(p, s)
            left_group(place, c)
            for p in place:
                right_part(p, c * PER, PER)

    for r in RINGS:
        pass_by(r).wait_send()

    @pl.loop(0, NS)
    def _(s):
        for r in RINGS:
            send(r, s, NEAR[r], OWN).wait_send()
            send(3 + r, s, FAR[r], r).wait_send()
        send(CORE, s, OTHER, OWN).wait_send()


def body(density, hamiltonian, left_operators, right_operators, block_mask, operator_slot, flip_sign, damping_rate, lower_weight):
    vmem, anywhere = (pl.BlockSpec(memory_space=m) for m in (pltpu.VMEM, pl.ANY))
    return pl.pallas_call(
        kernel,
        out_shape=pltpu.VMEM((1, 2, N, N), F32),
        in_specs=[anywhere] * 9,
        out_specs=vmem,
        scratch_shapes=[
            pltpu.VMEM((MODES + 1, NS, 2, SUB, N), BF16),
            pltpu.VMEM((3, 2, SUB, N), BF16),
            pltpu.VMEM((MODES + 1, 2, N, N), BF16),
            pltpu.VMEM((MODES + 1, 2, N, N), BF16),
            pltpu.VMEM((2, N, N), BF16),
            pltpu.VMEM((MODES, 2, NB, N), F32),
            pltpu.SMEM((MODES + 1,), F32),
            pltpu.SMEM((MODES + 1,), jnp.int32),
            pltpu.SMEM((MODES,), jnp.int32),
            pltpu.SMEM((MODES,), jnp.int32),
            pltpu.SMEM((MODES,), F32),
            pltpu.SMEM((MODES,), F32),
            pltpu.VMEM((MODES, 2, NB, NB), jnp.int32),
            pltpu.SemaphoreType.DMA((5,)),
            pltpu.SemaphoreType.DMA((NS,)),
            pltpu.SemaphoreType.DMA,
            pltpu.SemaphoreType.DMA((MODES,)),
            pltpu.SemaphoreType.DMA((MODES,)),
            pltpu.SemaphoreType.DMA((MODES, NS)),
            pltpu.SemaphoreType.DMA((MODES, NS)),
            pltpu.SemaphoreType.DMA((3,)),
            pltpu.SemaphoreType.DMA((3,)),
        ],
        compiler_params=pltpu.CompilerParams(
            collective_id=0, has_side_effects=True, vmem_limit_bytes=58 * 1024 * 1024),
        name="heom",
    )(operator_slot, flip_sign, damping_rate, lower_weight, block_mask, density, hamiltonian, left_operators, right_operators)


def solution(mesh):
    placed = (P(("wide", "narrow"), None, None, None), P(), P(), P(), P(), P(), P(), P(), P())
    return jax.shard_map(
        body, mesh=mesh, in_specs=placed, out_specs=P(("wide", "narrow"), None, None, None), check_vma=False)
```

```python
import jax
import jax.numpy as jnp
from jax import lax
from jax.experimental import pallas as pl
from jax.experimental.pallas import tpu as pltpu
from jax.sharding import PartitionSpec as P

MESH = pl.DeviceIdType.MESH
F32, BF16 = jnp.float32, jnp.bfloat16
N, BS, MODES, NB = 512, 64, 7, 8
CH = 128
NC = N // CH
SUB = 64
NS = N // SUB
PER = CH // SUB
MODE_AT = (0, 1, 4, 6, 2, 5, 3)
CORE, OWN = 6, 7
NEAR = ((0, 1), (0, 2), (2, 0))
FAR = ((8, 1), (0, 6), (6, 0))
OTHER = (1, 0)
LAST = NS - 1
LATE = NS - 2
ORDER = (0, LAST) + tuple(range(1, LAST))
RINGS = range(3)


def plan():
    def forward(s):
        return [("forward", None, s)]

    def steps(places, c):
        return [("step", p, c) for p in places]

    def group(places, c):
        return [("group", places, c)]

    near, far = (0, 1, 2), (3, 4, 5)
    out = [("step", OWN, c) for c in range(NC)] + forward(0)
    out += [("mask", None, s) for s in range(MODES)]
    out += steps([CORE], 0) + forward(1) + [("relay", 0, LAST)]
    out += steps([CORE], 1) + steps([CORE], 2) + steps([CORE], 3) + forward(2)
    out += group(near, 0) + forward(3)
    out += group(near, 1) + steps(far[:1], 0) + forward(4)
    out += group(far[1:], 0) + forward(5)
    out += group(near, 2) + steps(far[:1], 1) + forward(6)
    out += group(far[1:], 1) + [("late", 1, LATE)] + forward(7) + [("relay", 1, LAST)]
    out += group(near, 3) + group(far, 2) + group(far, 3)
    return out


PLAN = plan()


def kernel(
    slot_hbm, flip_hbm, rate_hbm, lower_hbm, mask_hbm, dens_hbm, ham_hbm, left_hbm, right_hbm, out_ref,
    rho, relay, left, right, ham, rows_ref, coef, slot_at, slot_ref, flip_ref, rate_ref, lower_ref, mask_ref,
    small_sem, dens_sem, ham_sem, left_sem, right_sem, send_sem, recv_sem, relay_send, relay_recv,
):
    wide, narrow = lax.axis_index("wide"), lax.axis_index("narrow")
    index = wide * 8 + narrow
    core = wide % 2
    acc = out_ref.at[0]

    def peer(masks):
        return (wide ^ masks[0], narrow ^ masks[1])

    barrier = pltpu.get_barrier_semaphore()
    peers = (OTHER,) + NEAR + FAR
    for masks in peers:
        pl.semaphore_signal(barrier, inc=1, device_id=peer(masks), device_id_type=MESH)

    dens = [
        pltpu.make_async_copy(
            dens_hbm.at[0, :, pl.ds(s * SUB, SUB), :], acc.at[:, pl.ds(s * SUB, SUB), :], dens_sem.at[s])
        for s in range(NS)
    ]
    for s in ORDER:
        dens[s].start()
    small = [
        pltpu.make_async_copy(src, dst, small_sem.at[i])
        for i, (src, dst) in enumerate((
            (rate_hbm, rate_ref), (flip_hbm, flip_ref), (lower_hbm, lower_ref), (slot_hbm, slot_ref), (mask_hbm, mask_ref)))
    ]
    for copy in small:
        copy.start()
    ham_copy = pltpu.make_async_copy(ham_hbm, ham, ham_sem)
    ham_copy.start()

    def load(s):
        return (
            pltpu.make_async_copy(left_hbm.at[s], left.at[s], left_sem.at[s]),
            pltpu.make_async_copy(right_hbm.at[s], right.at[s], right_sem.at[s]),
        )

    for copy in small[:4]:
        copy.wait()
    rate = jnp.float32(0.0)
    below = jnp.int32(0)
    for k in range(MODES):
        place = MODE_AT.index(k)
        bit = (index // 2**k) % 2
        parity = (1 - 2 * (below % 2)).astype(F32)
        sign = (1 - 2 * flip_ref[k]).astype(F32)
        on = bit.astype(F32)
        coef[place] = parity * sign * (on * lower_ref[k] + (1.0 - on))
        slot_at[place] = slot_ref[k]
        rate = rate + on * rate_ref[k]
        below = below + bit
    coef[OWN] = jnp.float32(1.0)

    def send(place, s, masks, src):
        return pltpu.make_async_remote_copy(
            src_ref=rho.at[src, s], dst_ref=rho.at[place, s],
            send_sem=send_sem.at[place, s], recv_sem=recv_sem.at[place, s],
            device_id=peer(masks), device_id_type=MESH)

    def pass_by(r):
        return pltpu.make_async_remote_copy(
            src_ref=rho.at[OWN, LAST], dst_ref=relay.at[r], send_sem=relay_send.at[r], recv_sem=relay_recv.at[r],
            device_id=peer(FAR[r]), device_id_type=MESH)

    def pass_on(r):
        return pltpu.make_async_remote_copy(
            src_ref=relay.at[r], dst_ref=rho.at[3 + r, LAST],
            send_sem=send_sem.at[3 + r, LAST], recv_sem=recv_sem.at[3 + r, LAST],
            device_id=peer(NEAR[r]), device_id_type=MESH)

    def send_near(s):
        for r in RINGS:
            send(r, s, NEAR[r], OWN).start()
        send(CORE, s, OTHER, OWN).start()

    def send_own(s):
        if s == LAST:
            for r in RINGS:
                pass_by(r).start()
        else:
            send_near(s)

    def forward(s):
        for r in RINGS:
            send(r, s, NEAR[r], OWN).wait_recv()
            if s == LATE:
                @pl.when(core == 0)
                def _():
                    send(3 + r, s, FAR[r], r).start()
            elif s != LAST:
                send(3 + r, s, FAR[r], r).start()

    for i, s in enumerate(ORDER):
        dens[s].wait()
        rows = pl.ds(s * SUB, SUB)
        value = acc[:, rows, :]
        rho[OWN, s] = value.astype(BF16)
        acc[:, rows, :] = (-rate) * value
        if i == 0:
            pl.semaphore_wait(barrier, len(peers))
        else:
            send_own(ORDER[i - 1])
        if i == NS // 2:
            for j in range(MODES):
                for copy in load(j):
                    copy.start()
    ham_copy.wait()
    left[OWN, 0] = ham[1]
    left[OWN, 1] = -ham[0]
    right[OWN, 0] = -ham[1]
    right[OWN, 1] = ham[0]
    send_own(ORDER[-1])
    send_near(LAST)

    small[4].wait()
    spread = (
        lax.broadcasted_iota(jnp.int32, (NB, N), 1) // BS == lax.broadcasted_iota(jnp.int32, (NB, N), 0)
    ).astype(F32)

    rows_ref[...] = jnp.dot(
        mask_ref[...].reshape(MODES * 2 * NB, NB).astype(F32), spread, preferred_element_type=F32
    ).reshape(MODES, 2, NB, N)

    def left_part(place, c):
        slot, weight = OWN if place == OWN else slot_at[place], coef[place]
        rows = pl.ds(c * CH, CH)
        both = jnp.concatenate([rho[place, c * PER + s, i] for i in range(2) for s in range(PER)], axis=0)
        lr, li = left[slot, 0, :, rows], left[slot, 1, :, rows]
        acc[0] += weight * jnp.dot(jnp.concatenate([lr, -li], axis=1), both, preferred_element_type=F32)
        acc[1] += weight * jnp.dot(jnp.concatenate([li, lr], axis=1), both, preferred_element_type=F32)

    def left_group(places, c):
        rows = pl.ds(c * CH, CH)
        real, imag = 0.0, 0.0
        for place in places:
            slot, weight = slot_at[place], coef[place]
            both = jnp.concatenate([rho[place, c * PER + s, i] for i in range(2) for s in range(PER)], axis=0)
            lr, li = left[slot, 0, :, rows], left[slot, 1, :, rows]
            real += weight * jnp.dot(jnp.concatenate([lr, -li], axis=1), both, preferred_element_type=F32)
            imag += weight * jnp.dot(jnp.concatenate([li, lr], axis=1), both, preferred_element_type=F32)
        acc[0] += real
        acc[1] += imag

    def right_part(place, first, count):
        slot, weight = OWN if place == OWN else slot_at[place], coef[place]
        rows = pl.ds(first * SUB, count * SUB)
        real, imag = (jnp.concatenate([rho[place, first + s, i] for s in range(count)], axis=0) for i in range(2))
        wide_rows = jnp.concatenate([
            jnp.concatenate([real, -imag], axis=1), jnp.concatenate([imag, real], axis=1)], axis=0)
        ops = jnp.concatenate([right[slot, 0], right[slot, 1]], axis=0)
        value = jnp.dot(wide_rows, ops, preferred_element_type=F32)
        acc[0, rows, :] += weight * value[: count * SUB]
        acc[1, rows, :] += weight * value[count * SUB :]

    def step(place, c):
        left_part(place, c)
        right_part(place, c * PER, PER)

    def mask(s):
        for copy in load(s):
            copy.wait()
        for i in range(NB):
            rows = pl.ds(i * BS, BS)
            for side, ops in ((0, left), (1, right)):
                keep = rows_ref[s, side, i : i + 1, :].astype(BF16)
                ops[s, 0, rows, :] = ops[s, 0, rows, :] * keep
                ops[s, 1, rows, :] = ops[s, 1, rows, :] * keep

    def arrived(place, s):
        if place == CORE:
            send(CORE, s, OTHER, OWN).wait_recv()
        elif place >= 3 and place != OWN:
            send(place, s, FAR[place - 3], place - 3).wait_recv()

    for what, place, c in PLAN:
        if what == "forward":
            forward(c)
        elif what == "late":
            @pl.when(core == 1)
            def _():
                for r in RINGS:
                    send(3 + r, c, FAR[r], r).start()
        elif what == "relay":
            @pl.when(core == place)
            def _():
                for r in RINGS:
                    pass_by(r).wait_recv()
                    pass_on(r).start()
        elif what == "mask":
            mask(c)
        elif what == "step":
            for s in range(c * PER, (c + 1) * PER):
                arrived(place, s)
            step(place, c)
        else:
            for p in place:
                for s in range(c * PER, (c + 1) * PER):
                    arrived(p, s)
            left_group(place, c)
            for p in place:
                right_part(p, c * PER, PER)

    for r in RINGS:
        pass_by(r).wait_send()

    @pl.loop(0, NS)
    def _(s):
        for r in RINGS:
            send(r, s, NEAR[r], OWN).wait_send()
            send(3 + r, s, FAR[r], r).wait_send()
        send(CORE, s, OTHER, OWN).wait_send()


def body(density, hamiltonian, left_operators, right_operators, block_mask, operator_slot, flip_sign, damping_rate, lower_weight):
    vmem, anywhere = (pl.BlockSpec(memory_space=m) for m in (pltpu.VMEM, pl.ANY))
    return pl.pallas_call(
        kernel,
        out_shape=pltpu.VMEM((1, 2, N, N), F32),
        in_specs=[anywhere] * 9,
        out_specs=vmem,
        scratch_shapes=[
            pltpu.VMEM((MODES + 1, NS, 2, SUB, N), BF16),
            pltpu.VMEM((3, 2, SUB, N), BF16),
            pltpu.VMEM((MODES + 1, 2, N, N), BF16),
            pltpu.VMEM((MODES + 1, 2, N, N), BF16),
            pltpu.VMEM((2, N, N), BF16),
            pltpu.VMEM((MODES, 2, NB, N), F32),
            pltpu.SMEM((MODES + 1,), F32),
            pltpu.SMEM((MODES + 1,), jnp.int32),
            pltpu.SMEM((MODES,), jnp.int32),
            pltpu.SMEM((MODES,), jnp.int32),
            pltpu.SMEM((MODES,), F32),
            pltpu.SMEM((MODES,), F32),
            pltpu.VMEM((MODES, 2, NB, NB), jnp.int32),
            pltpu.SemaphoreType.DMA((5,)),
            pltpu.SemaphoreType.DMA((NS,)),
            pltpu.SemaphoreType.DMA,
            pltpu.SemaphoreType.DMA((MODES,)),
            pltpu.SemaphoreType.DMA((MODES,)),
            pltpu.SemaphoreType.DMA((MODES, NS)),
            pltpu.SemaphoreType.DMA((MODES, NS)),
            pltpu.SemaphoreType.DMA((3,)),
            pltpu.SemaphoreType.DMA((3,)),
        ],
        compiler_params=pltpu.CompilerParams(
            collective_id=0, has_side_effects=True, vmem_limit_bytes=58 * 1024 * 1024),
        name="heom",
    )(operator_slot, flip_sign, damping_rate, lower_weight, block_mask, density, hamiltonian, left_operators, right_operators)


def solution(mesh):
    placed = (P(("wide", "narrow"), None, None, None), P(), P(), P(), P(), P(), P(), P(), P())
    return jax.shard_map(
        body, mesh=mesh, in_specs=placed, out_specs=P(("wide", "narrow"), None, None, None), check_vma=False)
```

```python
import jax
import jax.numpy as jnp
from jax import lax
from jax.experimental import pallas as pl
from jax.experimental.pallas import tpu as pltpu
from jax.sharding import PartitionSpec as P

MESH = pl.DeviceIdType.MESH
F32, BF16 = jnp.float32, jnp.bfloat16
N, BS, MODES, NB = 512, 64, 7, 8
CH = 128
NC = N // CH
SUB = 64
NS = N // SUB
PER = CH // SUB
MODE_AT = (0, 1, 4, 6, 2, 5, 3)
CORE, OWN = 6, 7
NEAR = ((0, 1), (0, 2), (2, 0))
FAR = ((8, 1), (0, 6), (6, 0))
OTHER = (1, 0)
LAST = NS - 1
LATE = (NS - 3, NS - 2)
ORDER = (0, LAST) + tuple(range(1, LAST))
RINGS = range(3)


def plan():
    def forward(s):
        return [("forward", None, s)]

    def steps(places, c):
        return [("step", p, c) for p in places]

    def group(places, c):
        return [("group", places, c)]

    near, far = (0, 1, 2), (3, 4, 5)
    out = [("step", OWN, c) for c in range(NC)] + forward(0)
    out += [("mask", None, s) for s in range(MODES)]
    out += steps([CORE], 0) + forward(1) + [("relay", 0, LAST)]
    out += steps([CORE], 1) + steps([CORE], 2) + steps([CORE], 3) + forward(2)
    out += group(near, 0) + forward(3)
    out += group(near, 1) + steps(far[:1], 0) + forward(4)
    out += group(far[1:], 0) + forward(5)
    out += group(near, 2) + [("late", 1, LATE[0])] + steps(far[:1], 1) + forward(6)
    out += group(far[1:], 1) + [("late", 1, LATE[1])] + forward(7) + [("relay", 1, LAST)]
    out += group(near, 3) + group(far, 2) + group(far, 3)
    return out


PLAN = plan()


def kernel(
    slot_hbm, flip_hbm, rate_hbm, lower_hbm, mask_hbm, dens_hbm, ham_hbm, left_hbm, right_hbm, out_ref,
    rho, relay, left, right, ham, rows_ref, coef, slot_at, slot_ref, flip_ref, rate_ref, lower_ref, mask_ref,
    small_sem, dens_sem, ham_sem, left_sem, right_sem, send_sem, recv_sem, relay_send, relay_recv,
):
    wide, narrow = lax.axis_index("wide"), lax.axis_index("narrow")
    index = wide * 8 + narrow
    core = wide % 2
    acc = out_ref.at[0]

    def peer(masks):
        return (wide ^ masks[0], narrow ^ masks[1])

    barrier = pltpu.get_barrier_semaphore()
    peers = (OTHER,) + NEAR + FAR
    for masks in peers:
        pl.semaphore_signal(barrier, inc=1, device_id=peer(masks), device_id_type=MESH)

    dens = [
        pltpu.make_async_copy(
            dens_hbm.at[0, :, pl.ds(s * SUB, SUB), :], acc.at[:, pl.ds(s * SUB, SUB), :], dens_sem.at[s])
        for s in range(NS)
    ]
    for s in ORDER:
        dens[s].start()
    small = [
        pltpu.make_async_copy(src, dst, small_sem.at[i])
        for i, (src, dst) in enumerate((
            (rate_hbm, rate_ref), (flip_hbm, flip_ref), (lower_hbm, lower_ref), (slot_hbm, slot_ref), (mask_hbm, mask_ref)))
    ]
    for copy in small:
        copy.start()
    ham_copy = pltpu.make_async_copy(ham_hbm, ham, ham_sem)
    ham_copy.start()

    def load(s):
        return (
            pltpu.make_async_copy(left_hbm.at[s], left.at[s], left_sem.at[s]),
            pltpu.make_async_copy(right_hbm.at[s], right.at[s], right_sem.at[s]),
        )

    for copy in small[:4]:
        copy.wait()
    rate = jnp.float32(0.0)
    below = jnp.int32(0)
    for k in range(MODES):
        place = MODE_AT.index(k)
        bit = (index // 2**k) % 2
        parity = (1 - 2 * (below % 2)).astype(F32)
        sign = (1 - 2 * flip_ref[k]).astype(F32)
        on = bit.astype(F32)
        coef[place] = parity * sign * (on * lower_ref[k] + (1.0 - on))
        slot_at[place] = slot_ref[k]
        rate = rate + on * rate_ref[k]
        below = below + bit
    coef[OWN] = jnp.float32(1.0)

    def send(place, s, masks, src):
        return pltpu.make_async_remote_copy(
            src_ref=rho.at[src, s], dst_ref=rho.at[place, s],
            send_sem=send_sem.at[place, s], recv_sem=recv_sem.at[place, s],
            device_id=peer(masks), device_id_type=MESH)

    def pass_by(r):
        return pltpu.make_async_remote_copy(
            src_ref=rho.at[OWN, LAST], dst_ref=relay.at[r], send_sem=relay_send.at[r], recv_sem=relay_recv.at[r],
            device_id=peer(FAR[r]), device_id_type=MESH)

    def pass_on(r):
        return pltpu.make_async_remote_copy(
            src_ref=relay.at[r], dst_ref=rho.at[3 + r, LAST],
            send_sem=send_sem.at[3 + r, LAST], recv_sem=recv_sem.at[3 + r, LAST],
            device_id=peer(NEAR[r]), device_id_type=MESH)

    def send_near(s):
        for r in RINGS:
            send(r, s, NEAR[r], OWN).start()
        send(CORE, s, OTHER, OWN).start()

    def send_own(s):
        if s == LAST:
            for r in RINGS:
                pass_by(r).start()
        else:
            send_near(s)

    def forward(s):
        for r in RINGS:
            send(r, s, NEAR[r], OWN).wait_recv()
            if s in LATE:
                @pl.when(core == 0)
                def _():
                    send(3 + r, s, FAR[r], r).start()
            elif s != LAST:
                send(3 + r, s, FAR[r], r).start()

    for i, s in enumerate(ORDER):
        dens[s].wait()
        rows = pl.ds(s * SUB, SUB)
        value = acc[:, rows, :]
        rho[OWN, s] = value.astype(BF16)
        acc[:, rows, :] = (-rate) * value
        if i == 0:
            pl.semaphore_wait(barrier, len(peers))
        else:
            send_own(ORDER[i - 1])
        if i == NS // 2:
            for j in range(MODES):
                for copy in load(j):
                    copy.start()
    ham_copy.wait()
    left[OWN, 0] = ham[1]
    left[OWN, 1] = -ham[0]
    right[OWN, 0] = -ham[1]
    right[OWN, 1] = ham[0]
    send_own(ORDER[-1])
    send_near(LAST)

    small[4].wait()
    spread = (
        lax.broadcasted_iota(jnp.int32, (NB, N), 1) // BS == lax.broadcasted_iota(jnp.int32, (NB, N), 0)
    ).astype(F32)

    rows_ref[...] = jnp.dot(
        mask_ref[...].reshape(MODES * 2 * NB, NB).astype(F32), spread, preferred_element_type=F32
    ).reshape(MODES, 2, NB, N)

    def left_part(place, c):
        slot, weight = OWN if place == OWN else slot_at[place], coef[place]
        rows = pl.ds(c * CH, CH)
        both = jnp.concatenate([rho[place, c * PER + s, i] for i in range(2) for s in range(PER)], axis=0)
        lr, li = left[slot, 0, :, rows], left[slot, 1, :, rows]
        acc[0] += weight * jnp.dot(jnp.concatenate([lr, -li], axis=1), both, preferred_element_type=F32)
        acc[1] += weight * jnp.dot(jnp.concatenate([li, lr], axis=1), both, preferred_element_type=F32)

    def left_group(places, c):
        rows = pl.ds(c * CH, CH)
        real, imag = 0.0, 0.0
        for place in places:
            slot, weight = slot_at[place], coef[place]
            both = jnp.concatenate([rho[place, c * PER + s, i] for i in range(2) for s in range(PER)], axis=0)
            lr, li = left[slot, 0, :, rows], left[slot, 1, :, rows]
            real += weight * jnp.dot(jnp.concatenate([lr, -li], axis=1), both, preferred_element_type=F32)
            imag += weight * jnp.dot(jnp.concatenate([li, lr], axis=1), both, preferred_element_type=F32)
        acc[0] += real
        acc[1] += imag

    def right_part(place, first, count):
        slot, weight = OWN if place == OWN else slot_at[place], coef[place]
        rows = pl.ds(first * SUB, count * SUB)
        real, imag = (jnp.concatenate([rho[place, first + s, i] for s in range(count)], axis=0) for i in range(2))
        wide_rows = jnp.concatenate([
            jnp.concatenate([real, -imag], axis=1), jnp.concatenate([imag, real], axis=1)], axis=0)
        ops = jnp.concatenate([right[slot, 0], right[slot, 1]], axis=0)
        value = jnp.dot(wide_rows, ops, preferred_element_type=F32)
        acc[0, rows, :] += weight * value[: count * SUB]
        acc[1, rows, :] += weight * value[count * SUB :]

    def step(place, c):
        left_part(place, c)
        right_part(place, c * PER, PER)

    def mask(s):
        for copy in load(s):
            copy.wait()
        for i in range(NB):
            rows = pl.ds(i * BS, BS)
            for side, ops in ((0, left), (1, right)):
                keep = rows_ref[s, side, i : i + 1, :].astype(BF16)
                ops[s, 0, rows, :] = ops[s, 0, rows, :] * keep
                ops[s, 1, rows, :] = ops[s, 1, rows, :] * keep

    def arrived(place, s):
        if place == CORE:
            send(CORE, s, OTHER, OWN).wait_recv()
        elif place >= 3 and place != OWN:
            send(place, s, FAR[place - 3], place - 3).wait_recv()

    for what, place, c in PLAN:
        if what == "forward":
            forward(c)
        elif what == "late":
            @pl.when(core == 1)
            def _():
                for r in RINGS:
                    send(3 + r, c, FAR[r], r).start()
        elif what == "relay":
            @pl.when(core == place)
            def _():
                for r in RINGS:
                    pass_by(r).wait_recv()
                    pass_on(r).start()
        elif what == "mask":
            mask(c)
        elif what == "step":
            for s in range(c * PER, (c + 1) * PER):
                arrived(place, s)
            step(place, c)
        else:
            for p in place:
                for s in range(c * PER, (c + 1) * PER):
                    arrived(p, s)
            left_group(place, c)
            for p in place:
                right_part(p, c * PER, PER)

    for r in RINGS:
        pass_by(r).wait_send()

    @pl.loop(0, NS)
    def _(s):
        for r in RINGS:
            send(r, s, NEAR[r], OWN).wait_send()
            send(3 + r, s, FAR[r], r).wait_send()
        send(CORE, s, OTHER, OWN).wait_send()


def body(density, hamiltonian, left_operators, right_operators, block_mask, operator_slot, flip_sign, damping_rate, lower_weight):
    vmem, anywhere = (pl.BlockSpec(memory_space=m) for m in (pltpu.VMEM, pl.ANY))
    return pl.pallas_call(
        kernel,
        out_shape=pltpu.VMEM((1, 2, N, N), F32),
        in_specs=[anywhere] * 9,
        out_specs=vmem,
        scratch_shapes=[
            pltpu.VMEM((MODES + 1, NS, 2, SUB, N), BF16),
            pltpu.VMEM((3, 2, SUB, N), BF16),
            pltpu.VMEM((MODES + 1, 2, N, N), BF16),
            pltpu.VMEM((MODES + 1, 2, N, N), BF16),
            pltpu.VMEM((2, N, N), BF16),
            pltpu.VMEM((MODES, 2, NB, N), F32),
            pltpu.SMEM((MODES + 1,), F32),
            pltpu.SMEM((MODES + 1,), jnp.int32),
            pltpu.SMEM((MODES,), jnp.int32),
            pltpu.SMEM((MODES,), jnp.int32),
            pltpu.SMEM((MODES,), F32),
            pltpu.SMEM((MODES,), F32),
            pltpu.VMEM((MODES, 2, NB, NB), jnp.int32),
            pltpu.SemaphoreType.DMA((5,)),
            pltpu.SemaphoreType.DMA((NS,)),
            pltpu.SemaphoreType.DMA,
            pltpu.SemaphoreType.DMA((MODES,)),
            pltpu.SemaphoreType.DMA((MODES,)),
            pltpu.SemaphoreType.DMA((MODES, NS)),
            pltpu.SemaphoreType.DMA((MODES, NS)),
            pltpu.SemaphoreType.DMA((3,)),
            pltpu.SemaphoreType.DMA((3,)),
        ],
        compiler_params=pltpu.CompilerParams(
            collective_id=0, has_side_effects=True, vmem_limit_bytes=58 * 1024 * 1024),
        name="heom",
    )(operator_slot, flip_sign, damping_rate, lower_weight, block_mask, density, hamiltonian, left_operators, right_operators)


def solution(mesh):
    placed = (P(("wide", "narrow"), None, None, None), P(), P(), P(), P(), P(), P(), P(), P())
    return jax.shard_map(
        body, mesh=mesh, in_specs=placed, out_specs=P(("wide", "narrow"), None, None, None), check_vma=False)
```
